32 devices in a mesh: ctx: 16 (over z, x, core), exp: 2 (over y).
Axes of the slice: x: 2, y: 2, z: 4, core: 2. Of those that a mesh axis runs over, the one named last changes fastest.
Arguments:
- resid: bfloat16 [2048, 2880], P(('ctx', 'exp')), may hold values from -3 to 3
- queries: bfloat16 [2048, 2048], P('ctx', 'exp'), may hold values from -8 to 8
- keys: bfloat16 [2048, 256], P('ctx'), may hold values from -8 to 8
- values: bfloat16 [2048, 256], P('ctx'), may hold values from -6 to 6
- sinks: float32 [32], P('exp'), may hold values from 0 to 6
- out_weight: bfloat16 [2048, 2880], P('exp'), may hold values from -0.125 to 0.125
- norm_gain: float32 [2880], replicated, may hold values from 0.5 to 1.5
- gate_weight: bfloat16 [16, 2880, 1536], P('ctx', None, 'exp'), may hold values from -0.109375 to 0.109375
- up_weight: bfloat16 [16, 2880, 1536], P('ctx', None, 'exp'), may hold values from -0.109375 to 0.109375
- down_weight: bfloat16 [16, 1536, 2880], P('ctx', 'exp'), may hold values from -0.15625 to 0.15625
- routes: int32 [2048, 4], P('ctx'), may hold values from 0 to 15, all different within a row; in each aligned block of 128 rows (0 to 127, 128 to 255, ...) at most 64 rows name the same one
- route_weights: float32 [2048, 4], P('ctx'), may hold values from 0.05 to 0.6
Outputs:
- block_out: bfloat16 [2048, 2880], P(('ctx', 'exp'))
The draws below stay inside these ranges and needn't reach their ends.
Inputs may be any that keep to these rules, and one draw needn't show every extreme that they name: `routes`: in each aligned block of 128 rows no expert is named by more than 64 rows, a bound that some block reaches; a row names 4 different experts.
All inputs are finite; a program needn't handle non-finite values.
Results may differ from the reference program's by a relative error of at most 0.0085.
Values may be sent and summed in bfloat16 or wider, within the bound.
A program may use at most 128 MiB of HBM per device.

```python
import math
import jax
import jax.numpy as jnp
import numpy as np
from jax import lax

D = 2880
HD = 64
QH = 32
KVH = 4
FFW = 1536
TOP = 4
WIN = 128
TOK_CTX = 128
SEQ = 2048
EXPERTS = 16
CAP = 64
N_CTX = 16
N_EXP = 2


def draw_queries(key, part):
    drawn = jnp.clip(jax.random.normal(jax.random.fold_in(key, 1), (SEQ, QH * HD), jnp.float32), -6.0, 6.0)
    return drawn.astype(jnp.bfloat16)


def draw_keys(key, part):
    drawn = jnp.clip(jax.random.normal(jax.random.fold_in(key, 3), (SEQ, KVH * HD), jnp.float32), -6.0, 6.0)
    return drawn.astype(jnp.bfloat16)


def steps_of(rng, extent, split, low, top_value):
    gain = 1.0
    for position, shards_of in split:
        heights = jax.random.uniform(jax.random.fold_in(jax.random.fold_in(rng, 6), position), (shards_of,), jnp.float32, low / len(split), top_value / len(split))
        gain = gain * jnp.repeat(jnp.exp(heights), extent[position] // shards_of).reshape((-1,) + (1,) * (len(extent) - 1 - position))
    return gain


def assign_block(rng, own, number, rows, count, top, bound, lean):
    order = jax.random.permutation(rng, count)
    crowded, usual = portions_of(count, rows * top, bound, lean, True), portions_of(count, rows * top, bound, lean, False)
    places = jnp.arange(count)

    def named(tallies, rotation):
        used = int((tallies > 0).sum())
        fixed = max(1, used // 4)
        shifted = fixed + (places - fixed + rotation * (used - fixed)) % max(1, count - fixed)
        return jnp.zeros((count,), jnp.int32).at[order[jnp.where(places < fixed, places, shifted)]].set(jnp.asarray(tallies, jnp.int32))

    tallies = jnp.where(number % 4 == 0, named(crowded, number // 4), named(usual, number - number // 4 - 1))
    mixed = jax.random.permutation(jax.random.fold_in(own, 3), count)
    donor, sink = mixed[0:count // 2 * 2:2], mixed[1:count // 2 * 2:2]
    room = jnp.minimum(tallies[donor] - 1, bound - tallies[sink]) // 2
    room = jnp.where((donor == order[0]) | (sink == order[0]) | (tallies[sink] == 0), 0, jnp.maximum(room, 0))
    shifted = jax.random.randint(jax.random.fold_in(own, 4), (count // 2,), 0, 1 << 20) % (room + 1)
    tallies = tallies.at[donor].add(-shifted).at[sink].add(shifted)
    labels = jnp.searchsorted(jnp.cumsum(tallies), jnp.arange(rows * top), side="right").astype(jnp.int32)
    table = labels.reshape(top, rows).T
    table = table[jax.random.permutation(jax.random.fold_in(own, 1), rows)]
    rotation = jax.random.randint(jax.random.fold_in(own, 2), (rows, 1), 0, top)
    return jnp.take_along_axis(table, (jnp.arange(top)[None, :] + rotation) % top, axis=1)


def portions_of(count, total, reach, skew, full):
    weights = [(1 << 20) // math.isqrt(grade ** skew) + 1 for grade in range(1, count + 1)]
    largest = reach if full else min(reach, max(-(-total // count), total * weights[0] // sum(weights)))
    least = 1 if total - largest >= count - 1 else 0
    holding, surplus = [largest] + [least] * (count - 1), total - largest - least * (count - 1)
    while surplus > 0:
        candidates = [i for i in range(1, count) if holding[i] < largest] or [i for i in range(1, count) if holding[i] < reach]
        pool, left = sum([weights[i] for i in candidates]), surplus
        for i in candidates:
            addition = min(reach - holding[i], max(1, left * weights[i] // pool), surplus)
            holding[i] = holding[i] + addition
            surplus = surplus - addition
    return np.array(holding)


def bell_draw(rng, dims, deviation, limit, shards=(), kind=jnp.bfloat16):
    array = deviation * jax.random.normal(rng, dims, jnp.float32)
    if shards:
        array = array * steps_of(rng, dims, shards, -0.22, 0.18)
    return jnp.clip(array, -limit, limit).astype(kind)


def setup_inputs(seed: int = 0) -> dict:
    seeds = jax.random.split(jax.random.key(seed), 13)
    resid = bell_draw(seeds[0], (SEQ, D), 0.5, 3.0, ((0, 32),))
    queries = draw_queries(jax.random.fold_in(seeds[12], 71), 0)
    keys = draw_keys(jax.random.fold_in(seeds[12], 71), 0)
    values = bell_draw(seeds[3], (SEQ, KVH * HD), 1.0, 6.0, ((0, 16),))
    sinks = jnp.clip(6.0 * jax.random.uniform(seeds[4], (QH,), jnp.float32) ** steps_of(seeds[4], (QH,), ((0, 2),), -0.2, 0.2), 0.0, 6.0)
    out_weight = bell_draw(seeds[5], (QH * HD, D), (QH * HD) ** -0.5, 0.125, ((0, 2),))
    norm_gain = jnp.clip(1.0 + 0.1 * jax.random.normal(seeds[6], (D,), jnp.float32), 0.5, 1.5)
    gate_weight = bell_draw(seeds[7], (EXPERTS, D, FFW), D ** -0.5, 0.109375, ((0, 16), (2, 2)))
    up_weight = bell_draw(seeds[8], (EXPERTS, D, FFW), D ** -0.5, 0.109375, ((0, 16), (2, 2)))
    down_weight = bell_draw(seeds[9], (EXPERTS, FFW, D), FFW ** -0.5, 0.15625, ((0, 16), (1, 2)))
    routes_keys = jax.random.split(jax.random.fold_in(seeds[10], 1), SEQ // TOK_CTX)
    routes_turns = jax.random.permutation(jax.random.fold_in(seeds[10], 3), SEQ // TOK_CTX)
    routes = jax.vmap(lambda own, number: assign_block(jax.random.fold_in(seeds[10], 2), own, number, TOK_CTX, EXPERTS, TOP, CAP, 2))(routes_keys, routes_turns).reshape((SEQ, TOP))
    route_weights = jnp.clip(0.05 + 0.55 * jax.random.uniform(seeds[11], (SEQ, TOP), jnp.float32) ** steps_of(seeds[11], (SEQ, TOP), ((0, 16),), -0.2, 0.2), 0.05, 0.6)
    return {"resid": resid, "queries": queries, "keys": keys, "values": values, "sinks": sinks, "out_weight": out_weight, "norm_gain": norm_gain, "gate_weight": gate_weight, "up_weight": up_weight, "down_weight": down_weight, "routes": routes, "route_weights": route_weights}


NEG_FILL = -1e+30
EPSILON = 1e-05

def attend_rows(q_rows, k_rows, v_rows, sinks, first_pos):
    per_group = QH // KVH
    query_four = q_rows.reshape(TOK_CTX, KVH, per_group, HD).astype(jnp.float32)
    key_three = k_rows.reshape(TOK_CTX + WIN, KVH, HD).astype(jnp.float32)
    value_three = v_rows.reshape(TOK_CTX + WIN, KVH, HD).astype(jnp.float32)
    scores = jnp.einsum('qgrd,kgd->grqk', query_four, key_three) * HD ** (-0.5)
    query_pos = first_pos + jnp.arange(TOK_CTX, dtype=jnp.int32)
    key_pos = first_pos - WIN + jnp.arange(TOK_CTX + WIN, dtype=jnp.int32)
    visible = (key_pos[None, :] <= query_pos[:, None]) & (key_pos[None, :] > query_pos[:, None] - WIN) & (key_pos[None, :] >= 0)
    masked = jnp.where(visible[None, None], scores, NEG_FILL)
    sink_cols = sinks.reshape(KVH, per_group)[:, :, None]
    row_max = jnp.maximum(lax.optimization_barrier(jnp.max(masked, axis=-1)), sink_cols)
    exp_terms = jnp.where(visible[None, None], jnp.exp(masked - row_max[..., None]), 0.0)
    denominator = lax.optimization_barrier(jnp.sum(exp_terms, axis=-1)) + jnp.exp(sink_cols - row_max)
    soft_weights = (exp_terms / denominator[..., None]).astype(jnp.bfloat16)
    attended_rows = jnp.einsum('grqk,kgd->qgrd', soft_weights.astype(jnp.float32), value_three)
    return attended_rows.reshape(TOK_CTX, QH * HD).astype(jnp.bfloat16)

def reference(resid, queries, keys, values, sinks, out_weight, norm_gain, gate_weight, up_weight, down_weight, routes, route_weights):
    zero_rows = jnp.zeros((WIN, KVH * HD), jnp.bfloat16)
    keys_padded = jnp.concatenate([zero_rows, keys], 0)
    values_padded = jnp.concatenate([zero_rows, values], 0)

    def one_block(block_id):
        first_pos = block_id * TOK_CTX
        q_rows = lax.dynamic_slice_in_dim(queries, first_pos, TOK_CTX, 0)
        k_rows = lax.dynamic_slice_in_dim(keys_padded, first_pos, TOK_CTX + WIN, 0)
        v_rows = lax.dynamic_slice_in_dim(values_padded, first_pos, TOK_CTX + WIN, 0)
        return attend_rows(q_rows, k_rows, v_rows, sinks, first_pos)
    attended = lax.map(one_block, jnp.arange(SEQ // TOK_CTX, dtype=jnp.int32)).reshape(SEQ, QH * HD)
    after_attention = resid.astype(jnp.float32) + jnp.dot(attended, out_weight, preferred_element_type=jnp.float32)
    mean_square = lax.optimization_barrier(jnp.mean(after_attention * after_attention, axis=-1, keepdims=True))
    normed = (after_attention * lax.rsqrt(mean_square + EPSILON) * norm_gain).astype(jnp.bfloat16)
    slot_total = N_CTX * CAP
    hidden_each = FFW // N_EXP

    def add_expert(carry, inputs):
        gate_w, up_w, down_w, expert_id = inputs
        hit = routes == expert_id
        token_weight = lax.optimization_barrier(jnp.sum(jnp.where(hit, route_weights, 0.0), axis=1))
        chosen = jnp.any(hit, axis=1)
        row_ids = jnp.nonzero(chosen, size=slot_total, fill_value=0)[0].astype(jnp.int32)
        live = (jnp.arange(slot_total, dtype=jnp.int32) < jnp.sum(chosen.astype(jnp.int32))).astype(jnp.float32)
        rows_in = normed[row_ids]
        gate_val = jnp.dot(rows_in, gate_w, preferred_element_type=jnp.float32)
        up_val = jnp.dot(rows_in, up_w, preferred_element_type=jnp.float32)
        activated = (jax.nn.silu(gate_val) * up_val).astype(jnp.bfloat16)
        pieces = jnp.einsum('rsh,shd->rsd', activated.reshape(slot_total, N_EXP, hidden_each).astype(jnp.float32), down_w.reshape(N_EXP, hidden_each, D).astype(jnp.float32))
        pieces = lax.optimization_barrier(pieces.astype(jnp.bfloat16)).astype(jnp.float32)
        contrib = lax.optimization_barrier(jnp.sum(pieces, axis=1)) * (token_weight[row_ids] * live)[:, None]
        return (carry.at[row_ids].add(contrib), None)
    start_mix = jnp.zeros((SEQ, D), jnp.float32)
    expert_mix, unused_out = lax.scan(add_expert, start_mix, (gate_weight, up_weight, down_weight, jnp.arange(EXPERTS, dtype=jnp.int32)))
    return (after_attention + expert_mix).astype(jnp.bfloat16)
```

```python
import jax
import jax.numpy as jnp
from jax import lax
from jax.sharding import PartitionSpec as P

HD = 64
QH = 32
KVH = 4
TOP = 4
WIN = 128


NEG_FILL = -1e30
EPSILON = 1e-05


def shifted(array, axis, by):
    size = lax.axis_size(axis)
    pairs = [(i, i + by) for i in range(size) if 0 <= i + by < size]
    return lax.ppermute(array, axis, pairs)


def flipped(array, bit):
    size = lax.axis_size("ctx")
    return lax.ppermute(array, "ctx", [(i, i ^ bit) for i in range(size)])


def swapped(array):
    return lax.ppermute(array, "exp", [(0, 1), (1, 0)])


def paired(mine, other, position, axis):
    low = jnp.where(position == 0, mine, other)
    high = jnp.where(position == 0, other, mine)
    return jnp.stack([low, high], axis)


def sum_halves(rows, position):
    half = rows.shape[0] // 2
    kept = lax.dynamic_slice_in_dim(rows, position * half, half, 0)
    sent = lax.dynamic_slice_in_dim(rows, (1 - position) * half, half, 0)
    return kept + swapped(sent.astype(jnp.bfloat16)).astype(jnp.float32)


def ranks(hit):
    count = hit.shape[1]
    places = jnp.arange(count)
    before = (places[:, None] < places[None, :]).astype(jnp.bfloat16)
    return jnp.dot(
        hit.astype(jnp.bfloat16), before, preferred_element_type=jnp.float32
    ).astype(jnp.int32)


def per_device_grouped(
    resid,
    queries,
    keys,
    values,
    sinks,
    out_weight,
    norm_gain,
    gate_weight,
    up_weight,
    down_weight,
    routes,
    route_weights,
):
    rows_here = queries.shape[0]
    local_heads = queries.shape[1] // HD
    per_group = QH // KVH
    kv_count = max(1, local_heads // per_group)
    head_reps = local_heads // kv_count
    exp_rank = lax.axis_index("exp")
    ctx_rank = lax.axis_index("ctx")
    kv_first = exp_rank * local_heads // per_group
    prior_keys, prior_values = shifted((keys, values), "ctx", 1)
    keys_ext = jnp.concatenate([prior_keys, keys], 0).reshape(rows_here + WIN, KVH, HD)
    values_ext = jnp.concatenate([prior_values, values], 0).reshape(rows_here + WIN, KVH, HD)
    keys_sel = lax.dynamic_slice_in_dim(keys_ext, kv_first, kv_count, 1)
    values_sel = lax.dynamic_slice_in_dim(values_ext, kv_first, kv_count, 1)
    query_four = queries.reshape(rows_here, kv_count, head_reps, HD)
    scores = jnp.einsum(
        "qgrd,kgd->grqk", query_four, keys_sel, preferred_element_type=jnp.float32
    ) * HD ** (-0.5)
    first_pos = ctx_rank * rows_here
    query_pos = first_pos + jnp.arange(rows_here, dtype=jnp.int32)
    key_pos = first_pos - WIN + jnp.arange(rows_here + WIN, dtype=jnp.int32)
    visible = (
        (key_pos[None, :] <= query_pos[:, None])
        & (key_pos[None, :] > query_pos[:, None] - WIN)
        & (key_pos[None, :] >= 0)
    )
    masked = jnp.where(visible[None, None], scores, NEG_FILL)
    sink_cols = sinks.reshape(kv_count, head_reps)[:, :, None]
    row_max = jnp.maximum(jnp.max(masked, axis=-1), sink_cols)
    exp_terms = jnp.where(visible[None, None], jnp.exp(masked - row_max[..., None]), 0.0)
    denominator = jnp.sum(exp_terms, axis=-1) + jnp.exp(sink_cols - row_max)
    soft_weights = (exp_terms / denominator[..., None]).astype(jnp.bfloat16)
    attended = jnp.einsum(
        "grqk,kgd->qgrd", soft_weights, values_sel, preferred_element_type=jnp.float32
    )
    attended = attended.reshape(rows_here, local_heads * HD).astype(jnp.bfloat16)
    width = out_weight.shape[1]
    own_rows = rows_here // 2
    n_experts = lax.axis_size("ctx")
    capacity = 2 * rows_here * TOP // n_experts
    table = jnp.concatenate([routes.astype(jnp.float32), route_weights], axis=1)
    tables = lax.all_gather(table, "ctx", axis=0)
    ids_all = tables[:, :, :TOP].astype(jnp.int32)
    weights_all = tables[:, :, TOP:]
    named = ids_all == ctx_rank
    hit_here = jnp.any(named, axis=2)
    weight_here = jnp.sum(jnp.where(named, weights_all, 0.0), axis=2)
    slots = jnp.arange(capacity, dtype=jnp.int32)
    pick = hit_here[:, None, :] & (ranks(hit_here)[:, None, :] == slots[None, :, None])
    slot_weight = jnp.sum(jnp.where(pick, weight_here[:, None, :], 0.0), axis=2)
    pick = pick.astype(jnp.bfloat16)
    hit_mine = jnp.any(routes[None, :, :] == jnp.arange(n_experts)[:, None, None], axis=2)
    place = hit_mine[:, :, None] & (ranks(hit_mine)[:, :, None] == slots[None, None, :])
    place = place.transpose(1, 0, 2).reshape(rows_here, n_experts * capacity).astype(jnp.bfloat16)

    projected = sum_halves(jnp.dot(attended, out_weight, preferred_element_type=jnp.float32), exp_rank)
    after_attention = resid.astype(jnp.float32) + projected
    mean_square = jnp.mean(after_attention * after_attention, axis=-1, keepdims=True)
    normed = (after_attention * lax.rsqrt(mean_square + EPSILON) * norm_gain).astype(jnp.bfloat16)

    core, x_pos, z_pos = ctx_rank % 2, ctx_rank // 2 % 2, ctx_rank // 4
    by_z = [normed] * 4
    for step in (1, -1):
        moving = normed
        for far in range(1, 4):
            moving = shifted(moving, "ctx", 4 * step)
            for z in range(4):
                by_z[z] = jnp.where(z_pos - step * far == z, moving, by_z[z])
    column = jnp.stack(by_z)
    first, second = column[:, : own_rows // 2], column[:, own_rows // 2 :]
    first = paired(first, flipped(first, 2), x_pos, 0)
    first = paired(first, swapped(first), exp_rank, 0)
    second = paired(second, swapped(second), exp_rank, 0)
    second = paired(second, flipped(second, 2), x_pos, 0)
    block = jnp.stack([first.transpose(2, 1, 0, 3, 4), second.transpose(2, 0, 1, 3, 4)], 3)
    block = block.reshape(n_experts // 2, rows_here, width)

    def expert_rows(tokens, owner):
        chosen = lax.dynamic_index_in_dim(
            pick.reshape(n_experts // 2, 2, capacity, rows_here), owner, 1, False
        )
        gains = lax.dynamic_index_in_dim(
            slot_weight.reshape(n_experts // 2, 2, capacity), owner, 1, False
        ).reshape(-1, 1)
        rows_in = jnp.einsum(
            "bst,btd->bsd", chosen, tokens, preferred_element_type=jnp.float32
        ).astype(jnp.bfloat16).reshape(-1, width)
        gate_val = jnp.dot(rows_in, gate_weight[0], preferred_element_type=jnp.float32)
        up_val = jnp.dot(rows_in, up_weight[0], preferred_element_type=jnp.float32)
        activated = (jax.nn.silu(gate_val) * up_val).astype(jnp.bfloat16)
        rows_out = jnp.dot(activated, down_weight[0], preferred_element_type=jnp.float32)
        return (rows_out * gains).astype(jnp.bfloat16).reshape(-1, capacity, width)

    other = flipped(block, 1)
    mine_out = expert_rows(block, core)
    other_out = expert_rows(other, 1 - core)
    outgoing = paired(mine_out, other_out, core, 1).reshape(n_experts, capacity, width)
    returned = lax.all_to_all(outgoing, "ctx", split_axis=0, concat_axis=0, tiled=True)
    combined = jnp.dot(
        place, returned.reshape(n_experts * capacity, width), preferred_element_type=jnp.float32
    )
    return (after_attention + sum_halves(combined, exp_rank)).astype(jnp.bfloat16)


def per_device(
    resid,
    queries,
    keys,
    values,
    sinks,
    out_weight,
    norm_gain,
    gate_weight,
    up_weight,
    down_weight,
    routes,
    route_weights,
):
    rows_here = queries.shape[0]
    local_heads = queries.shape[1] // HD
    per_group = QH // KVH
    kv_count = max(1, local_heads // per_group)
    head_reps = local_heads // kv_count
    exp_rank = lax.axis_index("exp")
    ctx_rank = lax.axis_index("ctx")
    kv_first = exp_rank * local_heads // per_group
    prior_keys, prior_values = shifted((keys, values), "ctx", 1)
    keys_ext = jnp.concatenate([prior_keys, keys], 0).reshape(rows_here + WIN, KVH, HD)
    values_ext = jnp.concatenate([prior_values, values], 0).reshape(rows_here + WIN, KVH, HD)
    keys_sel = lax.dynamic_slice_in_dim(keys_ext, kv_first, kv_count, 1)
    values_sel = lax.dynamic_slice_in_dim(values_ext, kv_first, kv_count, 1)
    query_four = queries.reshape(rows_here, kv_count, head_reps, HD)
    scores = jnp.einsum(
        "qgrd,kgd->grqk", query_four, keys_sel, preferred_element_type=jnp.float32
    ) * HD ** (-0.5)
    first_pos = ctx_rank * rows_here
    query_pos = first_pos + jnp.arange(rows_here, dtype=jnp.int32)
    key_pos = first_pos - WIN + jnp.arange(rows_here + WIN, dtype=jnp.int32)
    visible = (
        (key_pos[None, :] <= query_pos[:, None])
        & (key_pos[None, :] > query_pos[:, None] - WIN)
        & (key_pos[None, :] >= 0)
    )
    masked = jnp.where(visible[None, None], scores, NEG_FILL)
    sink_cols = sinks.reshape(kv_count, head_reps)[:, :, None]
    row_max = jnp.maximum(jnp.max(masked, axis=-1), sink_cols)
    exp_terms = jnp.where(visible[None, None], jnp.exp(masked - row_max[..., None]), 0.0)
    denominator = jnp.sum(exp_terms, axis=-1) + jnp.exp(sink_cols - row_max)
    soft_weights = (exp_terms / denominator[..., None]).astype(jnp.bfloat16)
    attended = jnp.einsum(
        "grqk,kgd->qgrd", soft_weights, values_sel, preferred_element_type=jnp.float32
    )
    attended = attended.reshape(rows_here, local_heads * HD).astype(jnp.bfloat16)
    projected = lax.psum_scatter(
        jnp.dot(attended, out_weight, preferred_element_type=jnp.float32),
        "exp",
        scatter_dimension=0,
        tiled=True,
    )
    after_attention = resid.astype(jnp.float32) + projected
    mean_square = jnp.mean(after_attention * after_attention, axis=-1, keepdims=True)
    normed = (after_attention * lax.rsqrt(mean_square + EPSILON) * norm_gain).astype(jnp.bfloat16)
    all_normed = lax.all_gather(normed, "exp", axis=0, tiled=True)
    n_experts = lax.axis_size("ctx")
    capacity = 2 * rows_here * TOP // n_experts
    width = all_normed.shape[1]
    flat_ids = routes.reshape(-1)
    one_hot = (flat_ids[:, None] == jnp.arange(n_experts, dtype=jnp.int32)[None, :]).astype(
        jnp.int32
    )
    rank_in = jnp.sum(jnp.cumsum(one_hot, axis=0) * one_hot, axis=1) - 1
    slot_index = flat_ids * capacity + rank_in
    token_of = jnp.arange(rows_here * TOP, dtype=jnp.int32) // TOP
    outgoing = (
        jnp.zeros((n_experts * capacity, width), jnp.bfloat16)
        .at[slot_index]
        .set(all_normed[token_of])
    )
    outgoing = outgoing.reshape(n_experts, capacity, width)
    gate_local = gate_weight[0]
    up_local = up_weight[0]
    down_local = down_weight[0]
    slot_block = lax.all_to_all(outgoing, "ctx", split_axis=0, concat_axis=0, tiled=True)
    block_shape = slot_block.shape
    flat_rows = slot_block.reshape(-1, block_shape[2])
    gate_val = jnp.dot(flat_rows, gate_local, preferred_element_type=jnp.float32)
    up_val = jnp.dot(flat_rows, up_local, preferred_element_type=jnp.float32)
    activated = (jax.nn.silu(gate_val) * up_val).astype(jnp.bfloat16)
    partial_rows = jnp.dot(activated, down_local, preferred_element_type=jnp.float32).astype(
        jnp.bfloat16
    )
    partial_out = partial_rows.reshape(block_shape)
    returned = lax.all_to_all(partial_out, "ctx", split_axis=0, concat_axis=0, tiled=True)
    flat_back = returned.reshape(n_experts * capacity, width)
    picked = flat_back[slot_index].reshape(rows_here, TOP, width)
    combined = jnp.sum(picked.astype(jnp.float32) * route_weights[:, :, None], axis=1)
    expert_mix = lax.psum_scatter(
        combined.astype(jnp.bfloat16), "exp", scatter_dimension=0, tiled=True
    ).astype(jnp.float32)
    return (after_attention + expert_mix).astype(jnp.bfloat16)


def solution(mesh):
    in_specs = (
        P(("ctx", "exp"), None),
        P("ctx", "exp"),
        P("ctx", None),
        P("ctx", None),
        P("exp"),
        P("exp", None),
        P(),
        P("ctx", None, "exp"),
        P("ctx", None, "exp"),
        P("ctx", "exp", None),
        P("ctx", None),
        P("ctx", None),
    )
    out_specs = P(("ctx", "exp"), None)
    grouped = mesh.shape["ctx"] == 16 and mesh.shape["exp"] == 2
    body = per_device_grouped if grouped else per_device
    return jax.shard_map(
        body, mesh=mesh, in_specs=in_specs, out_specs=out_specs, check_vma=False
    )
```
